32 devices in a mesh: gx: 4 (over x, core), gy: 8 (over z, y).
Axes of the slice: x: 2, y: 2, z: 4, core: 2. Of those that a mesh axis runs over, the one named last changes fastest.
Arguments:
- velocity: float32 [2, 11, 32, 1024], P(None, None, 'gx', 'gy'), may hold values from -6 to 6
- thickness: float32 [32, 1024], P('gx', 'gy'), may hold values from 0.5 to 2
- log_friction: float32 [32, 1024], P('gx', 'gy'), may hold values from -1 to 1
- obs_weight: float32 [32, 1024], P('gx', 'gy'), may hold values from 0.5 to 4
- ice_mask: int32 [32, 1024], P('gx', 'gy'), may hold values 0 or 1
- grounded: int32 [32, 1024], P('gx', 'gy'), may hold values 0 or 1
- probes: float32 [8, 32, 1024], P(None, 'gx', 'gy'), may hold values from -6 to 6
Outputs:
- hess_probe: float32 [8, 32, 1024], P(None, 'gx', 'gy')
The draws below stay inside these ranges and needn't reach their ends.
All inputs are finite; a program needn't handle non-finite values. No bound on the sum of `ice_mask` or of `grounded` on one device may be relied on, other than what follows from the above.
Results may differ from the reference program's by a relative error of at most 0.0003.
Values sent between devices are 32-bit elements; how exact they have to be, the bound alone decides.
A program may use at most 64 MiB of HBM per device.

```python
import math
import jax
import jax.numpy as jnp
from jax import lax

NL = 11
PROBES = 8
NX = 32
NY = 1024


def set_ends(values, key, least, largest):
    longest = values.shape.index(max(values.shape))
    spots = []
    for shift in (0, 1):
        where = [jax.random.randint(jax.random.fold_in(key, axis), (), 0, length) for axis, length in enumerate(values.shape)]
        where[longest] = (where[longest] + shift) % values.shape[longest]
        spots.append(tuple(where))
    return values.at[spots[0]].set(least).at[spots[1]].set(largest)


def level_of(rng, shape, shards, least, largest):
    loudness, own = 1.0, jax.random.fold_in(rng, 6)
    for dim, blocks in shards:
        steps = jnp.exp(jax.random.uniform(jax.random.fold_in(own, dim), (blocks,), jnp.float32, least / len(shards), largest / len(shards)))
        loudness = loudness * jnp.repeat(steps, shape[dim] // blocks).reshape([-1 if axis == dim else 1 for axis in range(len(shape))])
    return loudness


def centred(stream_key, dims, scale, limit, split=(), kind=jnp.bfloat16):
    drawn = jax.random.normal(stream_key, dims, jnp.float32) * scale
    if len(split) > 0:
        drawn = level_of(stream_key, dims, split, -0.22, 0.18) * drawn
    return jnp.clip(drawn, min=-limit, max=limit).astype(kind)


def setup_inputs(seed: int = 0) -> dict:
    key_list = jax.random.split(jax.random.key(seed), 8)
    return {
        "velocity": centred(key_list[0], (2, NL, NX, NY), 1.0, 6.0, ((2, 4), (3, 8)), jnp.float32),
        "thickness": jnp.clip(0.5 + 1.5 * jax.random.uniform(key_list[1], (NX, NY), jnp.float32) ** level_of(key_list[1], (NX, NY), ((0, 4), (1, 8)), -0.2, 0.2), 0.5, 2.0),
        "log_friction": jnp.clip(jax.random.uniform(key_list[2], (NX, NY), jnp.float32, -1.0, 1.0) * level_of(key_list[2], (NX, NY), ((0, 4), (1, 8)), -0.4, 0.0), -1.0, 1.0),
        "obs_weight": jnp.clip(jnp.exp(math.log(4.0) - 2.0794415 * jax.random.uniform(key_list[3], (NX, NY), jnp.float32) ** level_of(key_list[3], (NX, NY), ((0, 4), (1, 8)), -0.2, 0.2)), 0.5, 4.0),
        "ice_mask": set_ends((jax.random.randint(key_list[4], (NX, NY), 0, 4) < 3).astype(jnp.int32), jax.random.fold_in(key_list[4], 1), 0, 1),
        "grounded": set_ends((jax.random.randint(key_list[5], (NX, NY), 0, 3) < 2).astype(jnp.int32), jax.random.fold_in(key_list[5], 1), 0, 1),
        "probes": centred(key_list[6], (PROBES, NX, NY), 1.0, 6.0, ((1, 4), (2, 8)), jnp.float32),
    }


PRECISE = lax.Precision.HIGHEST
MASS_TERM = 0.1
STRAIN_OFFSET = 0.01

def viscosity(velocity_ext, thick_ext):
    layers = velocity_ext.shape[1]
    step_z = thick_ext[1:-1, 1:-1] / (layers - 1)
    speed_u = velocity_ext[0]
    speed_v = velocity_ext[1]
    grad_ux = 0.5 * (speed_u[:, 2:, 1:-1] - speed_u[:, :-2, 1:-1])
    grad_uy = 0.5 * (speed_u[:, 1:-1, 2:] - speed_u[:, 1:-1, :-2])
    grad_vx = 0.5 * (speed_v[:, 2:, 1:-1] - speed_v[:, :-2, 1:-1])
    grad_vy = 0.5 * (speed_v[:, 1:-1, 2:] - speed_v[:, 1:-1, :-2])
    middle = velocity_ext[:, :, 1:-1, 1:-1]
    column = jnp.concatenate([middle[:, :1], middle, middle[:, -1:]], axis=1)
    vertical_grad = (column[:, 2:] - column[:, :-2]) / (2.0 * step_z)
    strain = grad_ux * grad_ux + grad_vy * grad_vy + grad_ux * grad_vy + 0.25 * (grad_uy + grad_vx) ** 2 + 0.25 * (vertical_grad[0] ** 2 + vertical_grad[1] ** 2) + STRAIN_OFFSET
    return 0.5 * strain ** (-1.0 / 3.0)

def coefficients(visc_ext, mask_ext, thickness, grounded_f, log_friction):
    layers = visc_ext.shape[0]
    coef_x = 0.5 * (visc_ext[:, :-1, 1:-1] + visc_ext[:, 1:, 1:-1]) * (mask_ext[:-1, 1:-1] * mask_ext[1:, 1:-1])
    coef_y = 0.5 * (visc_ext[:, 1:-1, :-1] + visc_ext[:, 1:-1, 1:]) * (mask_ext[1:-1, :-1] * mask_ext[1:-1, 1:])
    interior = visc_ext[:, 1:-1, 1:-1]
    inverse_step = (layers - 1) / thickness
    coef_z = 0.5 * (interior[:-1] + interior[1:]) * (inverse_step * inverse_step)
    ice_own = mask_ext[1:-1, 1:-1]
    friction = ice_own * grounded_f * jnp.exp(log_friction)
    diag_base = MASS_TERM * ice_own + (1.0 - ice_own)
    zeros_upper = jnp.zeros((layers - 1,) + diag_base.shape, jnp.float32)
    diagonal = diag_base[None] + jnp.concatenate([friction[None], zeros_upper], axis=0)
    return (coef_x, coef_y, coef_z, diagonal, friction)

def anisotropy():
    aniso_x = jnp.array([4.0, 1.0], jnp.float32).reshape(2, 1, 1, 1)
    aniso_y = jnp.array([1.0, 4.0], jnp.float32).reshape(2, 1, 1, 1)
    return (aniso_x, aniso_y)

def operator_apply(extended, coef_x, coef_y, coef_z, diagonal):
    aniso_x, aniso_y = anisotropy()
    interior = extended[..., 1:-1, 1:-1]
    flux_x = coef_x * (extended[..., 1:, 1:-1] - extended[..., :-1, 1:-1])
    flux_y = coef_y * (extended[..., 1:-1, 1:] - extended[..., 1:-1, :-1])
    flux_z = coef_z * (interior[..., 1:, :, :] - interior[..., :-1, :, :])
    boundary_zero = jnp.zeros_like(flux_z[..., :1, :, :])
    vertical = jnp.concatenate([boundary_zero, flux_z], axis=-3) - jnp.concatenate([flux_z, boundary_zero], axis=-3)
    horizontal = aniso_x * (flux_x[..., :-1, :] - flux_x[..., 1:, :]) + aniso_y * (flux_y[..., :-1] - flux_y[..., 1:])
    return horizontal + vertical + diagonal * interior

def column_factors(coef_x, coef_y, coef_z, diagonal):
    aniso_x, aniso_y = anisotropy()
    layers = diagonal.shape[0]
    lateral = aniso_x * (coef_x[:, :-1] + coef_x[:, 1:]) + aniso_y * (coef_y[:, :, :-1] + coef_y[:, :, 1:])
    zero_layer = jnp.zeros_like(coef_z[:1])
    main_diag = lateral + diagonal + jnp.concatenate([zero_layer, coef_z], axis=0) + jnp.concatenate([coef_z, zero_layer], axis=0)
    ratios = []
    inverses = []
    for layer_index in range(layers):
        pivot_value = main_diag[:, layer_index]
        if layer_index > 0:
            pivot_value = pivot_value - coef_z[layer_index - 1] * ratios[-1]
        inverse = 1.0 / pivot_value
        inverses.append(inverse)
        if layer_index < layers - 1:
            ratios.append(coef_z[layer_index] * inverse)
    return (jnp.stack(ratios, axis=1), jnp.stack(inverses, axis=1))

def column_solve(residual, coef_z, ratios, inverses):
    layers = residual.shape[-3]
    forward_pass = []
    for layer_index in range(layers):
        current = residual[..., layer_index, :, :]
        if layer_index > 0:
            current = current + coef_z[layer_index - 1] * forward_pass[-1]
        forward_pass.append(current * inverses[:, layer_index])
    result = [forward_pass[-1]]
    for layer_index in range(layers - 2, -1, -1):
        result.append(forward_pass[layer_index] + ratios[:, layer_index] * result[-1])
    return jnp.stack(result[::-1], axis=-3)

def gram_matrix(left_block, right_block):
    probe_count = left_block.shape[0]
    return lax.dot_general(left_block.reshape(probe_count, -1), right_block.reshape(probe_count, -1), (((1,), (1,)), ((), ())), precision=PRECISE)

def combine(vectors, mixing):
    return jnp.tensordot(mixing, vectors, axes=((0,), (0,)), precision=PRECISE)

def small_solve(matrix, right_side):
    factor = jnp.linalg.cholesky(matrix)
    return jax.scipy.linalg.cho_solve((factor, True), right_side)

def block_solve(right_side, apply_fn, precond_fn):
    residual = right_side
    search = precond_fn(residual)
    norm_old = gram_matrix(residual, search)
    image = apply_fn(search)
    curvature = gram_matrix(search, image)
    step_mix = small_solve(curvature, norm_old)
    solution = combine(search, step_mix)
    residual = residual - combine(image, step_mix)
    precon = precond_fn(residual)
    norm_new = gram_matrix(residual, precon)
    update_mix = small_solve(norm_old, norm_new)
    search = precon + combine(search, update_mix)
    image = apply_fn(search)
    curvature = gram_matrix(search, image)
    step_mix = small_solve(curvature, norm_new)
    return solution + combine(search, step_mix)

def reference(velocity, thickness, log_friction, obs_weight, ice_mask, grounded, probes):
    layers = velocity.shape[1]
    mask_f = ice_mask.astype(jnp.float32)
    grounded_f = grounded.astype(jnp.float32)
    velocity_ext = jnp.pad(velocity, ((0, 0), (0, 0), (1, 1), (1, 1)))
    thick_ext = jnp.pad(thickness, 1, mode='edge')
    visc_node = viscosity(velocity_ext, thick_ext)
    visc_ext = jnp.pad(jnp.where(mask_f[None] > 0.5, visc_node, 0.0), ((0, 0), (1, 1), (1, 1)))
    mask_ext = jnp.pad(mask_f, 1)
    coef_x, coef_y, coef_z, diagonal, friction = coefficients(visc_ext, mask_ext, thickness, grounded_f, log_friction)
    ratios, inverses = column_factors(coef_x, coef_y, coef_z, diagonal)

    def apply_one(single):
        return operator_apply(jnp.pad(single, ((0, 0), (0, 0), (1, 1), (1, 1))), coef_x, coef_y, coef_z, diagonal)

    def apply_all(vectors):
        return lax.map(apply_one, vectors)

    def precond_all(vectors):
        return lax.map(lambda single: column_solve(single, coef_z, ratios, inverses), vectors)
    probe_count = probes.shape[0]
    upper_zero = jnp.zeros((probe_count, 2, layers - 1) + thickness.shape, jnp.float32)
    bottom = (friction[None] * probes)[:, None] * velocity[None, :, 0]
    forward_rhs = jnp.concatenate([bottom[:, :, None], upper_zero], axis=2)
    delta_u = block_solve(forward_rhs, apply_all, precond_all)
    surface = (obs_weight * mask_f)[None, None] * delta_u[:, :, layers - 1]
    adjoint_rhs = jnp.concatenate([upper_zero, surface[:, :, None]], axis=2)
    delta_lam = block_solve(adjoint_rhs, apply_all, precond_all)
    return friction[None] * jnp.sum(velocity[None, :, 0] * delta_lam[:, :, 0], axis=1)
```

```python
import functools

import jax
import jax.numpy as jnp
from jax import lax
from jax.experimental import pallas as pl
from jax.experimental.pallas import tpu as pltpu
from jax.sharding import PartitionSpec as P

MASS_TERM = 0.1
STRAIN_OFFSET = 0.01
ANISO_X = (4.0, 1.0)
ANISO_Y = (1.0, 4.0)
HIGHEST = lax.Precision.HIGHEST
MESH = pl.DeviceIdType.MESH
PAIR = 2


def round_up(value, step):
    return (value + step - 1) // step * step


def kernel(
    sizes,
    vel_ref, thick_ref, logf_ref, obs_ref, ice_ref, ground_ref, probes_ref,
    out_ref,
    xs1, xr1, ys1, yr1,
    xs2, xr2, ys2, yr2,
    xs3, xr3, ys3, yr3,
    ys4, yr4, ub,
    coef, kzs, ratio, inverse, green, weight, bext, bedge, uedge,
    fields, tile_src, ar_x, ar_y,
    send_sem, recv_sem, axs, axr, ays, ayr,
):
    n_gx, n_gy = sizes
    layers = vel_ref.shape[1]
    rows = vel_ref.shape[2]
    lanes = vel_ref.shape[3]
    probes = probes_ref.shape[0]
    half = probes // 2
    comps = 2 * layers
    last = layers - 1
    ix = lax.axis_index("gx")
    iy = lax.axis_index("gy")
    tile = (rows, lanes)
    lane = lax.broadcasted_iota(jnp.int32, tile, 1)
    sub = lax.broadcasted_iota(jnp.int32, tile, 0)
    slot = ((lane + 1) >> 1) & (lanes // 2 - 1)
    even = (lane & 1) == 0
    lane_first = lane == 0
    lane_last = lane == lanes - 1
    sub_first = sub == 0
    sub_last = sub == rows - 1

    barrier = pltpu.get_barrier_semaphore()
    for step in range(1, n_gx):
        pl.semaphore_signal(barrier, inc=1, device_id={"gx": lax.rem(ix + step, n_gx)}, device_id_type=MESH)
    for step in range(1, n_gy):
        pl.semaphore_signal(barrier, inc=1, device_id={"gy": lax.rem(iy + step, n_gy)}, device_id_type=MESH)

    def transfer(phase, way, src, dst):
        axis, idx, count = ("gx", ix, n_gx) if way < 2 else ("gy", iy, n_gy)
        down = way % 2 == 0
        has_dst = idx > 0 if down else idx < count - 1
        has_src = idx < count - 1 if down else idx > 0
        copy = pltpu.make_async_remote_copy(
            src_ref=src, dst_ref=dst,
            send_sem=send_sem.at[phase, way], recv_sem=recv_sem.at[phase, way],
            device_id={axis: idx - 1 if down else idx + 1}, device_id_type=MESH,
        )
        return copy, dst, has_dst, has_src

    def exchange(phase, x_src, x_dst, y_src, y_dst):
        return (
            transfer(phase, 0, x_src[0], x_dst[1]),
            transfer(phase, 1, x_src[1], x_dst[0]),
            transfer(phase, 2, y_src, y_dst[1]),
            transfer(phase, 3, y_src, y_dst[0]),
        )

    def clear(transfers):
        for _, dst, _, has_src in transfers:
            @pl.when(jnp.logical_not(has_src))
            def _(dst=dst):
                dst[...] = jnp.zeros(dst.shape, jnp.float32)

    def start(transfers):
        for copy, _, has_dst, _ in transfers:
            pl.when(has_dst)(copy.start)

    def finish(transfers):
        for copy, _, has_dst, has_src in transfers:
            pl.when(has_src)(copy.wait_recv)
        for copy, _, has_dst, has_src in transfers:
            pl.when(has_dst)(copy.wait_send)

    ex1 = exchange(0, (xs1.at[0], xs1.at[1]), (xr1.at[0], xr1.at[1]), ys1, (yr1.at[0], yr1.at[1]))
    ex2 = exchange(1, (xs2.at[0], xs2.at[1]), (xr2.at[0], xr2.at[1]), ys2, (yr2.at[0], yr2.at[1]))
    ex3 = exchange(2, (xs3.at[0], xs3.at[1]), (xr3.at[0], xr3.at[1]), ys3, (yr3.at[0], yr3.at[1]))
    ex45 = [
        exchange(
            3 + p,
            (ub.at[p, 1], ub.at[p, rows]), (ub.at[p, 0], ub.at[p, rows + 1]),
            ys4.at[p], (yr4.at[p, 0], yr4.at[p, 1]),
        )
        for p in range(2)
    ]

    def pack(tiles):
        packed = tiles[0]
        for m in range(1, len(tiles)):
            packed = jnp.where(slot == m, pltpu.roll(tiles[m], 2 * m, 1), packed)
        return packed

    def merge(south, north):
        return jnp.where(even, pltpu.roll(south, 1, 1), pltpu.roll(north, lanes - 1, 1))

    def unpack(merged, m):
        return merged if m == 0 else pltpu.roll(merged, lanes - 2 * m, 1)

    def west(t, row):
        return jnp.where(sub_first, row, pltpu.roll(t, 1, 0))

    def east(t, row):
        return jnp.where(sub_last, row, pltpu.roll(t, rows - 1, 0))

    def south(t, edge):
        return jnp.where(lane_first, edge, pltpu.roll(t, 1, 1))

    def north(t, edge):
        return jnp.where(lane_last, edge, pltpu.roll(t, lanes - 1, 1))

    def ahead(t, d):
        return t if d == 0 else pltpu.roll(t, probes - d, 0)

    mask = ice_ref[...].astype(jnp.float32)
    friction = mask * ground_ref[...].astype(jnp.float32) * jnp.exp(logf_ref[...])
    wm = obs_ref[...] * mask
    fields[0] = friction
    fields[1] = wm
    natural = [vel_ref[c, l] for c in range(2) for l in range(layers)] + [mask, wm]
    for k, t in enumerate(natural):
        xs1[0, k : k + 1, :] = t[0:1, :]
        xs1[1, k : k + 1, :] = t[rows - 1 : rows, :]
    base1 = round_up(len(natural), 8)
    drive = [friction * vel_ref[c, 0] for c in range(2)]
    for i in range(rows):
        probe = probes_ref[:, i, :]
        for c in range(2):
            bext[0, c, i + 1] = probe * drive[c][i : i + 1, :]
    for c in range(2):
        xs1[0, base1 + c * probes : base1 + (c + 1) * probes, :] = bext[0, c, 1]
        xs1[1, base1 + c * probes : base1 + (c + 1) * probes, :] = bext[0, c, rows]
    ys1[0:rows, :] = pack(natural)
    ys1[rows:, :] = pack([bext[0, c, i + 1] for c in range(2) for i in range(rows)])

    for ex in (ex1, ex2, ex3, ex45[0], ex45[1]):
        clear(ex)
    pl.semaphore_wait(barrier, n_gx + n_gy - 2)
    start(ex1)
    finish(ex1)

    merged1 = merge(yr1[0, 0:rows, :], yr1[1, 0:rows, :])
    edge1 = [unpack(merged1, k) for k in range(len(natural))]
    mergedb = merge(yr1[0, rows:, :], yr1[1, rows:, :])
    for c in range(2):
        bext[0, c, 0] = xr1[0, base1 + c * probes : base1 + (c + 1) * probes, :]
        bext[0, c, rows + 1] = xr1[1, base1 + c * probes : base1 + (c + 1) * probes, :]
        for i in range(rows):
            bedge[0, c, i] = unpack(mergedb, c * rows + i)

    def around(t, k):
        return (
            west(t, xr1[0, k : k + 1, :]), east(t, xr1[1, k : k + 1, :]),
            south(t, edge1[k]), north(t, edge1[k]),
        )

    inverse_step = last / thick_ref[...]
    half_step = 0.5 * inverse_step
    visc = []
    for l in range(layers):
        grads = []
        for c in range(2):
            w, e, s, n = around(vel_ref[c, l], c * layers + l)
            dz = (vel_ref[c, min(l + 1, last)] - vel_ref[c, max(l - 1, 0)]) * half_step
            grads.append((0.5 * (e - w), 0.5 * (n - s), dz))
        (ux, uy, uz), (vx, vy, vz) = grads
        shear = uy + vx
        strain = ux * ux + vy * vy + ux * vy + 0.25 * (shear * shear) + 0.25 * (uz * uz + vz * vz) + STRAIN_OFFSET
        root = jnp.exp(jnp.log(strain) * (-1.0 / 3.0))
        root = root + root * (1.0 - strain * root * root * root) * (1.0 / 3.0)
        mu = jnp.where(mask > 0.5, 0.5 * root, 0.0)
        visc.append(mu)
        xs2[0, l : l + 1, :] = mu[0:1, :]
        xs2[1, l : l + 1, :] = mu[rows - 1 : rows, :]
    ys2[...] = pack(visc)
    start(ex2)
    mask_w, mask_e, mask_s, mask_n = (0.5 * mask * m for m in around(mask, comps))
    step2 = inverse_step * inverse_step
    kz = [0.5 * (visc[l] + visc[l + 1]) * step2 for l in range(last)]
    for l in range(last):
        kzs[l] = kz[l]
    diag = MASS_TERM * mask + (1.0 - mask)
    finish(ex2)
    merged2 = merge(yr2[0], yr2[1])
    for l in range(layers):
        mu = visc[l]
        edge = unpack(merged2, l)
        coef[0, l] = (mu + west(mu, xr2[0, l : l + 1, :])) * mask_w
        coef[1, l] = (mu + east(mu, xr2[1, l : l + 1, :])) * mask_e
        coef[2, l] = (mu + south(mu, edge)) * mask_s
        coef[3, l] = (mu + north(mu, edge)) * mask_n

    for c in range(2):
        ratios, inverses = [], []
        for l in range(layers):
            pivot = ANISO_X[c] * (coef[0, l] + coef[1, l]) + ANISO_Y[c] * (coef[2, l] + coef[3, l]) + diag
            if l == 0:
                pivot = pivot + friction
            if l > 0:
                pivot = pivot + kz[l - 1]
            if l < last:
                pivot = pivot + kz[l]
            if l > 0:
                pivot = pivot - kz[l - 1] * ratios[-1]
            inv = 1.0 / pivot
            inverses.append(inv)
            inverse[c, l] = inv
            if l < last:
                ratios.append(kz[l] * inv)
                ratio[c, l] = ratios[-1]
        up = [inverses[0]]
        for l in range(1, layers):
            up.append(kz[l - 1] * up[-1] * inverses[l])
        low, top = up[last], inverses[last]
        for l in range(last, -1, -1):
            if l < last:
                low = up[l] + ratios[l] * low
                top = ratios[l] * top
            green[0, c, l] = low
            green[1, c, l] = top
    tiles3 = []
    for p in range(2):
        for c in range(2):
            for l in range(layers):
                k = len(tiles3)
                t = green[p, c, l]
                tiles3.append(t)
                xs3[0, k : k + 1, :] = t[0:1, :]
                xs3[1, k : k + 1, :] = t[rows - 1 : rows, :]
    ys3[...] = pack(tiles3)
    start(ex3)
    finish(ex3)
    merged3 = merge(yr3[0], yr3[1])
    for p in range(2):
        for c in range(2):
            for l in range(layers):
                k = (p * 2 + c) * layers + l
                t = green[p, c, l]
                edge = unpack(merged3, k)
                weight[p, c, 0, l] = ANISO_X[c] * coef[0, l] * west(t, xr3[0, k : k + 1, :])
                weight[p, c, 1, l] = ANISO_X[c] * coef[1, l] * east(t, xr3[1, k : k + 1, :])
                weight[p, c, 2, l] = ANISO_Y[c] * coef[2, l] * south(t, edge)
                weight[p, c, 3, l] = ANISO_Y[c] * coef[3, l] * north(t, edge)

    zero = jnp.zeros((probes, lanes), jnp.float32)

    def outer(acc, left, right):
        return tuple(acc[d] + left * ahead(right, d) for d in range(half + 1))

    def solve(p):
        src = 0 if p == 0 else last
        dst = last - src

        def first(t, accs):
            acc_s, acc_1, acc_2 = accs
            packed = None
            for ii in range(PAIR):
                i = t * PAIR + ii
                for c in range(2):
                    b0 = bext[p, c, i + 1]
                    bw = bext[p, c, i]
                    be = bext[p, c, i + 2]
                    edge = bedge[p, c, i]
                    bs = south(b0, edge)
                    bn = north(b0, edge)
                    lateral, y = [], []
                    for l in range(layers):
                        n1 = (
                            weight[p, c, 0, l, pl.ds(i, 1), :] * bw
                            + weight[p, c, 1, l, pl.ds(i, 1), :] * be
                            + weight[p, c, 2, l, pl.ds(i, 1), :] * bs
                            + weight[p, c, 3, l, pl.ds(i, 1), :] * bn
                        )
                        lateral.append(n1)
                        if l > 0:
                            n1 = n1 + kzs[l - 1, pl.ds(i, 1), :] * y[-1]
                        y.append(n1 * inverse[c, l, pl.ds(i, 1), :])
                    x = y[last]
                    for l in range(last, -1, -1):
                        if l < last:
                            x = y[l] + ratio[c, l, pl.ds(i, 1), :] * x
                        ub[p, i + 1, c * layers + l] = x
                        m = (ii * 2 + c) * layers + l
                        moved = x if m == 0 else pltpu.roll(x, 2 * m, 1)
                        packed = moved if packed is None else jnp.where(slot == m, moved, packed)
                        acc_2 = outer(acc_2, lateral[l], x)
                        if l == src:
                            acc_1 = outer(acc_1, b0, x)
                    acc_s = outer(acc_s, green[p, c, src, pl.ds(i, 1), :] * b0, b0)
            ys4[p, pl.ds(pl.multiple_of(t * rows, rows), rows), :] = packed
            return acc_s, acc_1, acc_2

        none = (zero,) * (half + 1)
        acc_s, acc_1, acc_2 = lax.fori_loop(0, rows // PAIR, first, (none, none, none))
        start(ex45[p])
        finish(ex45[p])

        def second(t, acc_3):
            at = pl.ds(pl.multiple_of(t * rows, rows), rows)
            merged = merge(yr4[p, 0, at, :], yr4[p, 1, at, :])
            for ii in range(PAIR):
                i = t * PAIR + ii
                for l in range(layers):
                    cw, ce, cs, cn = (coef[q, l, pl.ds(i, 1), :] for q in range(4))
                    for c in range(2):
                        k = c * layers + l
                        w0 = ub[p, i + 1, k]
                        edge = unpack(merged, ii * comps + k)
                        if l == dst:
                            uedge[c, i] = edge
                        n2 = ANISO_X[c] * (cw * ub[p, i, k] + ce * ub[p, i + 2, k]) + ANISO_Y[c] * (
                            cs * south(w0, edge) + cn * north(w0, edge)
                        )
                        acc_3 = outer(acc_3, n2, w0)
            return acc_3

        acc_3 = lax.fori_loop(0, rows // PAIR, second, none)

        grams = jnp.zeros((probes, lanes), jnp.float32)
        for g, acc in enumerate((acc_s, acc_1, acc_2, acc_3)):
            for d in range(half + 1):
                total = jnp.broadcast_to(jnp.sum(acc[d], axis=1, keepdims=True), (probes, lanes))
                grams = jnp.where(lane == g * probes + (sub + d) % probes, total, grams)
                if 0 < d < half:
                    moved = pltpu.roll(total, d, 0)
                    grams = jnp.where(lane == g * probes + (sub + probes - d) % probes, moved, grams)

        def reduce_axis(value, stage, axis, idx, count, landed, ssem, rsem):
            tile_src[p, stage] = value
            copies = [
                pltpu.make_async_remote_copy(
                    src_ref=tile_src.at[p, stage], dst_ref=landed.at[p, d - 1],
                    send_sem=ssem.at[p, d - 1], recv_sem=rsem.at[p, d - 1],
                    device_id={axis: lax.rem(idx + d, count)}, device_id_type=MESH,
                )
                for d in range(1, count)
            ]
            for copy in copies:
                copy.start()
            for d, copy in enumerate(copies):
                copy.wait_recv()
                value = value + landed[p, d]
            for copy in copies:
                copy.wait_send()
            return value

        grams = reduce_axis(grams, 0, "gx", ix, n_gx, ar_x, axs, axr)
        grams = reduce_axis(grams, 1, "gy", iy, n_gy, ar_y, ays, ayr)

        diff = grams - pltpu.roll(grams, lanes - probes, 1)
        upper = jnp.where(lane < 2 * probes, diff, pltpu.roll(grams, 2 * probes, 1))
        lower = jnp.where(lane < 2 * probes, pltpu.roll(diff, lanes - probes, 1), pltpu.roll(grams, probes, 1))
        size = 2 * probes
        both = [upper, lower]
        scale = [jnp.sum(jnp.where(lane == sub + h * probes, both[h], 0.0), axis=1, keepdims=True) for h in range(2)]
        for k in range(size):
            h, r = k // probes, k % probes
            row = both[h][r : r + 1, :]
            pivot = row[:, k : k + 1]
            inv = jnp.where(pivot > 1e-6 * scale[h][r : r + 1, :], 1.0 / pivot, 0.0)
            row = row * inv
            for q in range(2):
                updated = both[q] - both[q][:, k : k + 1] * row
                both[q] = jnp.where(sub == r, row, updated) if q == h else updated
        pick = (lane == sub + size).astype(jnp.float32)
        return lax.dot_general(
            pick, jnp.concatenate(both, axis=0), (((1,), (1,)), ((), ())),
            precision=HIGHEST, preferred_element_type=jnp.float32,
        )

    def mix(mixing, pairs):
        stacked = jnp.concatenate([jnp.concatenate(pair, axis=0) for pair in pairs], axis=1)
        mixed = lax.dot_general(
            mixing, stacked, (((1,), (0,)), ((), ())), precision=HIGHEST, preferred_element_type=jnp.float32
        )
        return [mixed[:, k * lanes : (k + 1) * lanes] for k in range(len(pairs))]

    mixing = solve(0)
    wm_edge = edge1[comps + 1]
    for c in range(2):
        k = c * layers + last
        inner = green[0, c, last]
        edge = unpack(merged3, k)
        pairs = [(xr3[0, k : k + 1, :] * bext[0, c, 0], ub[0, 0, k])]
        pairs += [(inner[i : i + 1, :] * bext[0, c, i + 1], ub[0, i + 1, k]) for i in range(rows)]
        pairs += [(xr3[1, k : k + 1, :] * bext[0, c, rows + 1], ub[0, rows + 1, k])]
        pairs += [(edge[i : i + 1, :] * bedge[0, c, i], uedge[c, i]) for i in range(rows)]
        mixed = mix(mixing, pairs)
        bext[1, c, 0] = mixed[0] * xr1[0, comps + 1 : comps + 2, :]
        bext[1, c, rows + 1] = mixed[rows + 1] * xr1[1, comps + 1 : comps + 2, :]
        for i in range(rows):
            bext[1, c, i + 1] = mixed[i + 1] * wm[i : i + 1, :]
            bedge[1, c, i] = mixed[rows + 2 + i] * wm_edge[i : i + 1, :]

    mixing = solve(1)
    results = []
    for c in range(2):
        inner = green[1, c, 0]
        results.append(mix(mixing, [
            (inner[i : i + 1, :] * bext[1, c, i + 1], ub[1, i + 1, c * layers]) for i in range(rows)
        ]))
    for i in range(rows):
        out_ref[:, i, :] = drive[0][i : i + 1, :] * results[0][i] + drive[1][i : i + 1, :] * results[1][i]


def body(sizes, velocity, thickness, log_friction, obs_weight, ice_mask, grounded, probes):
    layers, rows, lanes = velocity.shape[1:]
    count = probes.shape[0]
    comps = 2 * layers
    n_gx, n_gy = sizes
    rows1 = round_up(comps + 2, 8) + 2 * count
    rows2 = round_up(layers, 8)
    rows3 = round_up(2 * comps, 8)
    packs = rows // PAIR * count

    def vmem(*shape):
        return pltpu.VMEM(shape, jnp.float32)

    def borders(x_rows, y_rows):
        return [vmem(2, x_rows, lanes), vmem(2, x_rows, lanes), vmem(y_rows, lanes), vmem(2, y_rows, lanes)]

    sem = pltpu.SemaphoreType.DMA
    scratch = (
        borders(rows1, rows + count)
        + borders(rows2, rows)
        + borders(rows3, rows)
        + [vmem(2, packs, lanes), vmem(2, 2, packs, lanes), vmem(2, rows + 2, comps, count, lanes)]
        + [
            vmem(4, layers, rows, lanes), vmem(layers - 1, rows, lanes),
            vmem(2, layers - 1, rows, lanes), vmem(2, layers, rows, lanes),
            vmem(2, 2, layers, rows, lanes), vmem(2, 2, 4, layers, rows, lanes),
            vmem(2, 2, rows + 2, count, lanes), vmem(2, 2, rows, count, lanes), vmem(2, rows, count, lanes),
            vmem(2, rows, lanes), vmem(2, 2, count, lanes),
            vmem(2, n_gx - 1, count, lanes), vmem(2, n_gy - 1, count, lanes),
        ]
        + [sem((5, 4)), sem((5, 4)), sem((2, n_gx - 1)), sem((2, n_gx - 1)), sem((2, n_gy - 1)), sem((2, n_gy - 1))]
    )
    return pl.pallas_call(
        functools.partial(kernel, sizes),
        out_shape=jax.ShapeDtypeStruct(probes.shape, jnp.float32),
        in_specs=[pl.BlockSpec(memory_space=pltpu.VMEM)] * 7,
        out_specs=pl.BlockSpec(memory_space=pltpu.VMEM),
        scratch_shapes=scratch,
        compiler_params=pltpu.CompilerParams(collective_id=0, has_side_effects=True),
        name="hessian_probe",
    )(velocity, thickness, log_friction, obs_weight, ice_mask, grounded, probes)


def solution(mesh):
    sizes = (mesh.shape["gx"], mesh.shape["gy"])
    in_specs = (
        P(None, None, "gx", "gy"),
        P("gx", "gy"),
        P("gx", "gy"),
        P("gx", "gy"),
        P("gx", "gy"),
        P("gx", "gy"),
        P(None, "gx", "gy"),
    )
    out_specs = P(None, "gx", "gy")
    return jax.shard_map(
        functools.partial(body, sizes), mesh=mesh, in_specs=in_specs, out_specs=out_specs, check_vma=False
    )
```

```python
import functools

import jax
import jax.numpy as jnp
from jax import lax
from jax.experimental import pallas as pl
from jax.experimental.pallas import tpu as pltpu
from jax.sharding import PartitionSpec as P

MASS_TERM = 0.1
STRAIN_OFFSET = 0.01
ANISO_X = (4.0, 1.0)
ANISO_Y = (1.0, 4.0)
HIGHEST = lax.Precision.HIGHEST
MESH = pl.DeviceIdType.MESH
PAIR = 2


def round_up(value, step):
    return (value + step - 1) // step * step


def kernel(
    sizes,
    vel_ref, thick_ref, logf_ref, obs_ref, ice_ref, ground_ref, probes_ref,
    out_ref,
    xs1, xr1, ys1, yr1,
    xs2, xr2, ys2, yr2,
    xs3, xr3, ys3, yr3,
    ys4, yr4, ub,
    coef, kzs, ratio, inverse, green, weight, bext, bedge, uedge,
    fields, tile_src, ar_x, ar_y,
    send_sem, recv_sem, axs, axr, ays, ayr,
):
    n_gx, n_gy = sizes
    layers = vel_ref.shape[1]
    rows = vel_ref.shape[2]
    lanes = vel_ref.shape[3]
    probes = probes_ref.shape[0]
    half = probes // 2
    comps = 2 * layers
    last = layers - 1
    ix = lax.axis_index("gx")
    iy = lax.axis_index("gy")
    tile = (rows, lanes)
    lane = lax.broadcasted_iota(jnp.int32, tile, 1)
    sub = lax.broadcasted_iota(jnp.int32, tile, 0)
    slot = ((lane + 1) >> 1) & (lanes // 2 - 1)
    even = (lane & 1) == 0
    lane_first = lane == 0
    lane_last = lane == lanes - 1
    sub_first = sub == 0
    sub_last = sub == rows - 1

    sent = []
    barrier = pltpu.get_barrier_semaphore()
    for step in range(1, n_gx):
        pl.semaphore_signal(barrier, inc=1, device_id={"gx": lax.rem(ix + step, n_gx)}, device_id_type=MESH)
    for step in range(1, n_gy):
        pl.semaphore_signal(barrier, inc=1, device_id={"gy": lax.rem(iy + step, n_gy)}, device_id_type=MESH)

    def transfer(phase, way, src, dst):
        axis, idx, count = ("gx", ix, n_gx) if way < 2 else ("gy", iy, n_gy)
        down = way % 2 == 0
        has_dst = idx > 0 if down else idx < count - 1
        has_src = idx < count - 1 if down else idx > 0
        copy = pltpu.make_async_remote_copy(
            src_ref=src, dst_ref=dst,
            send_sem=send_sem.at[phase, way], recv_sem=recv_sem.at[phase, way],
            device_id={axis: idx - 1 if down else idx + 1}, device_id_type=MESH,
        )
        return copy, dst, has_dst, has_src

    def exchange(phase, x_src, x_dst, y_src, y_dst):
        return (
            transfer(phase, 0, x_src[0], x_dst[1]),
            transfer(phase, 1, x_src[1], x_dst[0]),
            transfer(phase, 2, y_src, y_dst[1]),
            transfer(phase, 3, y_src, y_dst[0]),
        )

    def clear(transfers):
        for _, dst, _, has_src in transfers:
            @pl.when(jnp.logical_not(has_src))
            def _(dst=dst):
                dst[...] = jnp.zeros(dst.shape, jnp.float32)

    def start(transfers):
        for copy, _, has_dst, _ in transfers:
            pl.when(has_dst)(copy.start)

    def finish(transfers):
        for copy, _, has_dst, has_src in transfers:
            pl.when(has_src)(copy.wait_recv)
        sent.extend((copy, has_dst) for copy, _, has_dst, _ in transfers)

    ex1 = exchange(0, (xs1.at[0], xs1.at[1]), (xr1.at[0], xr1.at[1]), ys1, (yr1.at[0], yr1.at[1]))
    ex2 = exchange(1, (xs2.at[0], xs2.at[1]), (xr2.at[0], xr2.at[1]), ys2, (yr2.at[0], yr2.at[1]))
    ex3 = exchange(2, (xs3.at[0], xs3.at[1]), (xr3.at[0], xr3.at[1]), ys3, (yr3.at[0], yr3.at[1]))
    pairs_of_rows = rows // PAIR
    ex_rows = [
        (transfer(3 + p, 0, ub.at[p, 1], ub.at[p, rows + 1]), transfer(3 + p, 1, ub.at[p, rows], ub.at[p, 0]))
        for p in range(2)
    ]
    ex_packs = [
        [
            tuple(
                transfer(
                    3 + p + 2 * t, 2 + w, ys4.at[p, pl.ds(t * probes, probes)],
                    yr4.at[p, 1 - w, pl.ds(t * probes, probes)],
                )
                for w in range(2)
            )
            for t in range(pairs_of_rows)
        ]
        for p in range(2)
    ]

    def pack(tiles):
        packed = tiles[0]
        for m in range(1, len(tiles)):
            packed = jnp.where(slot == m, pltpu.roll(tiles[m], 2 * m, 1), packed)
        return packed

    def merge(south, north):
        return jnp.where(even, pltpu.roll(south, 1, 1), pltpu.roll(north, lanes - 1, 1))

    def unpack(merged, m):
        return merged if m == 0 else pltpu.roll(merged, lanes - 2 * m, 1)

    def west(t, row):
        return jnp.where(sub_first, row, pltpu.roll(t, 1, 0))

    def east(t, row):
        return jnp.where(sub_last, row, pltpu.roll(t, rows - 1, 0))

    def south(t, edge):
        return jnp.where(lane_first, edge, pltpu.roll(t, 1, 1))

    def north(t, edge):
        return jnp.where(lane_last, edge, pltpu.roll(t, lanes - 1, 1))

    def ahead(t, d):
        return t if d == 0 else pltpu.roll(t, probes - d, 0)

    mask = ice_ref[...].astype(jnp.float32)
    friction = mask * ground_ref[...].astype(jnp.float32) * jnp.exp(logf_ref[...])
    wm = obs_ref[...] * mask
    fields[0] = friction
    fields[1] = wm
    natural = [vel_ref[c, l] for c in range(2) for l in range(layers)] + [mask, wm]
    for k, t in enumerate(natural):
        xs1[0, k : k + 1, :] = t[0:1, :]
        xs1[1, k : k + 1, :] = t[rows - 1 : rows, :]
    base1 = round_up(len(natural), 8)
    drive = [friction * vel_ref[c, 0] for c in range(2)]
    for i in range(rows):
        probe = probes_ref[:, i, :]
        for c in range(2):
            bext[0, c, i + 1] = probe * drive[c][i : i + 1, :]
    for c in range(2):
        xs1[0, base1 + c * probes : base1 + (c + 1) * probes, :] = bext[0, c, 1]
        xs1[1, base1 + c * probes : base1 + (c + 1) * probes, :] = bext[0, c, rows]
    ys1[0:rows, :] = pack(natural)
    ys1[rows:, :] = pack([bext[0, c, i + 1] for c in range(2) for i in range(rows)])

    for ex in [ex1, ex2, ex3] + ex_rows + ex_packs[0] + ex_packs[1]:
        clear(ex)
    pl.semaphore_wait(barrier, n_gx + n_gy - 2)
    start(ex1)
    finish(ex1)

    merged1 = merge(yr1[0, 0:rows, :], yr1[1, 0:rows, :])
    edge1 = [unpack(merged1, k) for k in range(len(natural))]
    mergedb = merge(yr1[0, rows:, :], yr1[1, rows:, :])
    for c in range(2):
        bext[0, c, 0] = xr1[0, base1 + c * probes : base1 + (c + 1) * probes, :]
        bext[0, c, rows + 1] = xr1[1, base1 + c * probes : base1 + (c + 1) * probes, :]
        for i in range(rows):
            bedge[0, c, i] = unpack(mergedb, c * rows + i)

    def around(t, k):
        return (
            west(t, xr1[0, k : k + 1, :]), east(t, xr1[1, k : k + 1, :]),
            south(t, edge1[k]), north(t, edge1[k]),
        )

    inverse_step = last / thick_ref[...]
    half_step = 0.5 * inverse_step
    visc = []
    for l in range(layers):
        grads = []
        for c in range(2):
            w, e, s, n = around(vel_ref[c, l], c * layers + l)
            dz = (vel_ref[c, min(l + 1, last)] - vel_ref[c, max(l - 1, 0)]) * half_step
            grads.append((0.5 * (e - w), 0.5 * (n - s), dz))
        (ux, uy, uz), (vx, vy, vz) = grads
        shear = uy + vx
        strain = ux * ux + vy * vy + ux * vy + 0.25 * (shear * shear) + 0.25 * (uz * uz + vz * vz) + STRAIN_OFFSET
        root = jnp.exp(jnp.log(strain) * (-1.0 / 3.0))
        root = root + root * (1.0 - strain * root * root * root) * (1.0 / 3.0)
        mu = jnp.where(mask > 0.5, 0.5 * root, 0.0)
        visc.append(mu)
        xs2[0, l : l + 1, :] = mu[0:1, :]
        xs2[1, l : l + 1, :] = mu[rows - 1 : rows, :]
    ys2[...] = pack(visc)
    start(ex2)
    mask_w, mask_e, mask_s, mask_n = (0.5 * mask * m for m in around(mask, comps))
    step2 = inverse_step * inverse_step
    kz = [0.5 * (visc[l] + visc[l + 1]) * step2 for l in range(last)]
    for l in range(last):
        kzs[l] = kz[l]
    diag = MASS_TERM * mask + (1.0 - mask)
    finish(ex2)
    merged2 = merge(yr2[0], yr2[1])
    for l in range(layers):
        mu = visc[l]
        edge = unpack(merged2, l)
        coef[0, l] = (mu + west(mu, xr2[0, l : l + 1, :])) * mask_w
        coef[1, l] = (mu + east(mu, xr2[1, l : l + 1, :])) * mask_e
        coef[2, l] = (mu + south(mu, edge)) * mask_s
        coef[3, l] = (mu + north(mu, edge)) * mask_n

    for c in range(2):
        ratios, inverses = [], []
        for l in range(layers):
            pivot = ANISO_X[c] * (coef[0, l] + coef[1, l]) + ANISO_Y[c] * (coef[2, l] + coef[3, l]) + diag
            if l == 0:
                pivot = pivot + friction
            if l > 0:
                pivot = pivot + kz[l - 1]
            if l < last:
                pivot = pivot + kz[l]
            if l > 0:
                pivot = pivot - kz[l - 1] * ratios[-1]
            inv = 1.0 / pivot
            inverses.append(inv)
            inverse[c, l] = inv
            if l < last:
                ratios.append(kz[l] * inv)
                ratio[c, l] = ratios[-1]
        up = [inverses[0]]
        for l in range(1, layers):
            up.append(kz[l - 1] * up[-1] * inverses[l])
        low, top = up[last], inverses[last]
        for l in range(last, -1, -1):
            if l < last:
                low = up[l] + ratios[l] * low
                top = ratios[l] * top
            green[0, c, l] = low
            green[1, c, l] = top
    tiles3 = []
    for p in range(2):
        for c in range(2):
            for l in range(layers):
                k = len(tiles3)
                t = green[p, c, l]
                tiles3.append(t)
                xs3[0, k : k + 1, :] = t[0:1, :]
                xs3[1, k : k + 1, :] = t[rows - 1 : rows, :]
    ys3[...] = pack(tiles3)
    start(ex3)
    finish(ex3)
    merged3 = merge(yr3[0], yr3[1])
    for p in range(2):
        for c in range(2):
            for l in range(layers):
                k = (p * 2 + c) * layers + l
                t = green[p, c, l]
                edge = unpack(merged3, k)
                weight[p, c, 0, l] = ANISO_X[c] * coef[0, l] * west(t, xr3[0, k : k + 1, :])
                weight[p, c, 1, l] = ANISO_X[c] * coef[1, l] * east(t, xr3[1, k : k + 1, :])
                weight[p, c, 2, l] = ANISO_Y[c] * coef[2, l] * south(t, edge)
                weight[p, c, 3, l] = ANISO_Y[c] * coef[3, l] * north(t, edge)

    zero = jnp.zeros((probes, lanes), jnp.float32)

    def outer(acc, left, right):
        return tuple(acc[d] + left * ahead(right, d) for d in range(half + 1))

    def place(grams, g, acc):
        for d in range(half + 1):
            total = jnp.broadcast_to(jnp.sum(acc[d], axis=1, keepdims=True), (probes, lanes))
            grams = jnp.where(lane == g * probes + (sub + d) % probes, total, grams)
            if 0 < d < half:
                moved = pltpu.roll(total, d, 0)
                grams = jnp.where(lane == g * probes + (sub + probes - d) % probes, moved, grams)
        return grams

    def solve(p):
        src = 0 if p == 0 else last
        dst = last - src

        def first(t, accs):
            acc_s, acc_1, acc_2 = accs
            packed = None
            for ii in range(PAIR):
                i = t * PAIR + ii
                for c in range(2):
                    b0 = bext[p, c, i + 1]
                    bw = bext[p, c, i]
                    be = bext[p, c, i + 2]
                    edge = bedge[p, c, i]
                    bs = south(b0, edge)
                    bn = north(b0, edge)
                    lateral, y = [], []
                    for l in range(layers):
                        n1 = (
                            weight[p, c, 0, l, pl.ds(i, 1), :] * bw
                            + weight[p, c, 1, l, pl.ds(i, 1), :] * be
                            + weight[p, c, 2, l, pl.ds(i, 1), :] * bs
                            + weight[p, c, 3, l, pl.ds(i, 1), :] * bn
                        )
                        lateral.append(n1)
                        if l > 0:
                            n1 = n1 + kzs[l - 1, pl.ds(i, 1), :] * y[-1]
                        y.append(n1 * inverse[c, l, pl.ds(i, 1), :])
                    x = y[last]
                    for l in range(last, -1, -1):
                        if l < last:
                            x = y[l] + ratio[c, l, pl.ds(i, 1), :] * x
                        ub[p, i + 1, c * layers + l] = x
                        m = (ii * 2 + c) * layers + l
                        moved = x if m == 0 else pltpu.roll(x, 2 * m, 1)
                        packed = moved if packed is None else jnp.where(slot == m, moved, packed)
                        acc_2 = outer(acc_2, lateral[l], x)
                        if l == src:
                            acc_1 = outer(acc_1, b0, x)
                    acc_s = outer(acc_s, green[p, c, src, pl.ds(i, 1), :] * b0, b0)
            ys4[p, pl.ds(t * probes, probes), :] = packed
            return acc_s, acc_1, acc_2

        none = (zero,) * (half + 1)
        accs = (none, none, none)
        order = [0, pairs_of_rows - 1] + list(range(1, pairs_of_rows - 1))
        for n, t in enumerate(order):
            accs = first(t, accs)
            start(ex_packs[p][t])
            if n == 1:
                start(ex_rows[p])
        grams = jnp.zeros((probes, lanes), jnp.float32)
        for g in range(3):
            grams = place(grams, g, accs[g])
        for t in order:
            finish(ex_packs[p][t])
        finish(ex_rows[p])

        def second(t, acc_3):
            at = pl.ds(pl.multiple_of(t * probes, probes), probes)
            merged = merge(yr4[p, 0, at, :], yr4[p, 1, at, :])
            for ii in range(PAIR):
                i = t * PAIR + ii
                for l in range(layers):
                    cw, ce, cs, cn = (coef[q, l, pl.ds(i, 1), :] for q in range(4))
                    for c in range(2):
                        k = c * layers + l
                        w0 = ub[p, i + 1, k]
                        edge = unpack(merged, ii * comps + k)
                        if l == dst:
                            uedge[c, i] = edge
                        n2 = ANISO_X[c] * (cw * ub[p, i, k] + ce * ub[p, i + 2, k]) + ANISO_Y[c] * (
                            cs * south(w0, edge) + cn * north(w0, edge)
                        )
                        acc_3 = outer(acc_3, n2, w0)
            return acc_3

        acc_3 = lax.fori_loop(0, rows // PAIR, second, none)

        grams = place(grams, 3, acc_3)

        def reduce_axis(value, stage, axis, idx, count, landed, ssem, rsem):
            tile_src[p, stage] = value
            copies = [
                pltpu.make_async_remote_copy(
                    src_ref=tile_src.at[p, stage], dst_ref=landed.at[p, d - 1],
                    send_sem=ssem.at[p, d - 1], recv_sem=rsem.at[p, d - 1],
                    device_id={axis: lax.rem(idx + d, count)}, device_id_type=MESH,
                )
                for d in range(1, count)
            ]
            for copy in copies:
                copy.start()
            for d, copy in enumerate(copies):
                copy.wait_recv()
                value = value + landed[p, d]
            sent.extend((copy, None) for copy in copies)
            return value

        grams = reduce_axis(grams, 0, "gx", ix, n_gx, ar_x, axs, axr)
        grams = reduce_axis(grams, 1, "gy", iy, n_gy, ar_y, ays, ayr)

        diff = grams - pltpu.roll(grams, lanes - probes, 1)
        upper = jnp.where(lane < 2 * probes, diff, pltpu.roll(grams, 2 * probes, 1))
        lower = jnp.where(lane < 2 * probes, pltpu.roll(diff, lanes - probes, 1), pltpu.roll(grams, probes, 1))
        size = 2 * probes
        both = [upper, lower]
        scale = [jnp.sum(jnp.where(lane == sub + h * probes, both[h], 0.0), axis=1, keepdims=True) for h in range(2)]
        for k in range(size):
            h, r = k // probes, k % probes
            row = both[h][r : r + 1, :]
            pivot = row[:, k : k + 1]
            inv = jnp.where(pivot > 1e-6 * scale[h][r : r + 1, :], 1.0 / pivot, 0.0)
            row = row * inv
            for q in range(2):
                updated = both[q] - both[q][:, k : k + 1] * row
                both[q] = jnp.where(sub == r, row, updated) if q == h else updated
        pick = (lane == sub + size).astype(jnp.float32)
        return lax.dot_general(
            pick, jnp.concatenate(both, axis=0), (((1,), (1,)), ((), ())),
            precision=HIGHEST, preferred_element_type=jnp.float32,
        )

    def mix(mixing, pairs):
        stacked = jnp.concatenate([jnp.concatenate(pair, axis=0) for pair in pairs], axis=1)
        mixed = lax.dot_general(
            mixing, stacked, (((1,), (0,)), ((), ())), precision=HIGHEST, preferred_element_type=jnp.float32
        )
        return [mixed[:, k * lanes : (k + 1) * lanes] for k in range(len(pairs))]

    mixing = solve(0)
    wm_edge = edge1[comps + 1]
    for c in range(2):
        k = c * layers + last
        inner = green[0, c, last]
        edge = unpack(merged3, k)
        pairs = [(xr3[0, k : k + 1, :] * bext[0, c, 0], ub[0, 0, k])]
        pairs += [(inner[i : i + 1, :] * bext[0, c, i + 1], ub[0, i + 1, k]) for i in range(rows)]
        pairs += [(xr3[1, k : k + 1, :] * bext[0, c, rows + 1], ub[0, rows + 1, k])]
        pairs += [(edge[i : i + 1, :] * bedge[0, c, i], uedge[c, i]) for i in range(rows)]
        mixed = mix(mixing, pairs)
        bext[1, c, 0] = mixed[0] * xr1[0, comps + 1 : comps + 2, :]
        bext[1, c, rows + 1] = mixed[rows + 1] * xr1[1, comps + 1 : comps + 2, :]
        for i in range(rows):
            bext[1, c, i + 1] = mixed[i + 1] * wm[i : i + 1, :]
            bedge[1, c, i] = mixed[rows + 2 + i] * wm_edge[i : i + 1, :]

    mixing = solve(1)
    results = []
    for c in range(2):
        inner = green[1, c, 0]
        results.append(mix(mixing, [
            (inner[i : i + 1, :] * bext[1, c, i + 1], ub[1, i + 1, c * layers]) for i in range(rows)
        ]))
    for i in range(rows):
        out_ref[:, i, :] = drive[0][i : i + 1, :] * results[0][i] + drive[1][i : i + 1, :] * results[1][i]
    for copy, has_dst in sent:
        if has_dst is None:
            copy.wait_send()
        else:
            pl.when(has_dst)(copy.wait_send)


def body(sizes, velocity, thickness, log_friction, obs_weight, ice_mask, grounded, probes):
    layers, rows, lanes = velocity.shape[1:]
    count = probes.shape[0]
    comps = 2 * layers
    n_gx, n_gy = sizes
    rows1 = round_up(comps + 2, 8) + 2 * count
    rows2 = round_up(layers, 8)
    rows3 = round_up(2 * comps, 8)
    packs = rows // PAIR * count

    def vmem(*shape):
        return pltpu.VMEM(shape, jnp.float32)

    def borders(x_rows, y_rows):
        return [vmem(2, x_rows, lanes), vmem(2, x_rows, lanes), vmem(y_rows, lanes), vmem(2, y_rows, lanes)]

    sem = pltpu.SemaphoreType.DMA
    scratch = (
        borders(rows1, rows + count)
        + borders(rows2, rows)
        + borders(rows3, rows)
        + [vmem(2, packs, lanes), vmem(2, 2, packs, lanes), vmem(2, rows + 2, comps, count, lanes)]
        + [
            vmem(4, layers, rows, lanes), vmem(layers - 1, rows, lanes),
            vmem(2, layers - 1, rows, lanes), vmem(2, layers, rows, lanes),
            vmem(2, 2, layers, rows, lanes), vmem(2, 2, 4, layers, rows, lanes),
            vmem(2, 2, rows + 2, count, lanes), vmem(2, 2, rows, count, lanes), vmem(2, rows, count, lanes),
            vmem(2, rows, lanes), vmem(2, 2, count, lanes),
            vmem(2, n_gx - 1, count, lanes), vmem(2, n_gy - 1, count, lanes),
        ]
        + [sem((3 + 2 * (rows // PAIR), 4)), sem((3 + 2 * (rows // PAIR), 4)), sem((2, n_gx - 1)), sem((2, n_gx - 1)), sem((2, n_gy - 1)), sem((2, n_gy - 1))]
    )
    return pl.pallas_call(
        functools.partial(kernel, sizes),
        out_shape=jax.ShapeDtypeStruct(probes.shape, jnp.float32),
        in_specs=[pl.BlockSpec(memory_space=pltpu.VMEM)] * 7,
        out_specs=pl.BlockSpec(memory_space=pltpu.VMEM),
        scratch_shapes=scratch,
        compiler_params=pltpu.CompilerParams(collective_id=0, has_side_effects=True),
        name="hessian_probe",
    )(velocity, thickness, log_friction, obs_weight, ice_mask, grounded, probes)


def solution(mesh):
    sizes = (mesh.shape["gx"], mesh.shape["gy"])
    in_specs = (
        P(None, None, "gx", "gy"),
        P("gx", "gy"),
        P("gx", "gy"),
        P("gx", "gy"),
        P("gx", "gy"),
        P("gx", "gy"),
        P(None, "gx", "gy"),
    )
    out_specs = P(None, "gx", "gy")
    return jax.shard_map(
        functools.partial(body, sizes), mesh=mesh, in_specs=in_specs, out_specs=out_specs, check_vma=False
    )
```
